32 devices in a mesh: gz: 16 (over z, y, x), col: 2 (over core).
Axes of the slice: x: 2, y: 2, z: 4, core: 2. Of those that a mesh axis runs over, the one named last changes fastest.
Arguments:
- velocity: float32 [64, 3, 128, 128], P('gz', None, 'col'), may hold values from -6 to 6
- forces: float32 [3, 131072], P(None, ('gz', 'col')), may hold values from -60 to 60
- offsets: float32 [3, 131072], P(None, ('gz', 'col')), may hold values from 0 to 1
- cell_x: int32 [131072], P(('gz', 'col')), may hold values from 0 to 127
- cell_y: int32 [131072], P(('gz', 'col')), may hold values from 0 to 127
- cell_z: int32 [131072], P(('gz', 'col')), may hold values from 0 to 12
- band_start: int32 [16], P('gz'), may hold values from 0 to 15, as said below
Outputs:
- force_field: float32 [64, 3, 128, 128], P('gz', None, 'col')
- velocity_next: float32 [64, 3, 128, 128], P('gz', None, 'col')
The draws below stay inside these ranges and needn't reach their ends.
Inputs may be any that keep to these rules, and one draw needn't show every extreme that they name: (g - band_start[g]) mod 16 lies in 0 to 3 for every gz index g.
All inputs are finite; a program needn't handle non-finite values.
Results may differ from the reference program's by a relative error of at most 0.0037.
Values sent between devices are 32-bit elements; how exact they have to be, the bound alone decides.
A program may use at most 64 MiB of HBM per device.

```python
import jax
import jax.numpy as jnp
from jax import lax

CZ = 4
NX = 128
NY = 128
MK_DEV = 4096
BAND = 4
BANDZ = 16
NZ = 64
MARKERS = 131072
N_GZ = 16
N_COL = 2


def draw_band_start(key, part):
    backward = jax.random.randint(key, (N_GZ,), 0, BAND)
    backward = backward.at[0].set(0).at[1].set(BAND - 1)
    return ((jnp.arange(N_GZ, dtype=jnp.int32) - backward) % N_GZ).astype(jnp.int32)


def with_ends(entries, key, smallest, high):
    spot = [jax.random.randint(jax.random.fold_in(key, axis), (), 0, length) for axis, length in enumerate(entries.shape)]
    longest = entries.shape.index(max(entries.shape))
    next_to = spot[:longest] + [(spot[longest] + 1) % entries.shape[longest]] + spot[longest + 1:]
    return entries.at[tuple(spot)].set(smallest).at[tuple(next_to)].set(high)


def levels(own_key, extent, shards, least, largest):
    factor_of, own = 1.0, jax.random.fold_in(own_key, 6)
    for position, shards_of in shards:
        steps = jnp.exp(jax.random.uniform(jax.random.fold_in(own, position), (shards_of,), jnp.float32, least / len(shards), largest / len(shards)))
        factor_of = factor_of * jnp.repeat(steps, extent[position] // shards_of).reshape([-1 if axis == position else 1 for axis in range(len(extent))])
    return factor_of


def normal_values(rng, dims, scale, reach, cuts=(), held_as=jnp.bfloat16):
    result = jax.random.normal(rng, dims, jnp.float32) * scale
    if len(cuts) > 0:
        result = levels(rng, dims, cuts, -0.22, 0.18) * result
    return jnp.clip(result, min=-reach, max=reach).astype(held_as)


def setup_inputs(seed: int = 0) -> dict:
    arg_keys = jax.random.split(jax.random.key(seed), 8)
    velocity = normal_values(arg_keys[0], (NZ, 3, NX, NY), 1.0, 6.0, ((0, 16), (2, 2)), jnp.float32)
    forces = normal_values(arg_keys[1], (3, MARKERS), 10.0, 60.0, ((1, 32),), jnp.float32)
    offsets = jnp.clip(1.0 * jax.random.uniform(arg_keys[2], (3, MARKERS), jnp.float32) ** levels(arg_keys[2], (3, MARKERS), ((1, 32),), -0.2, 0.2), 0.0, 1.0)
    cell_x = with_ends(jax.random.randint(arg_keys[3], (MARKERS,), 0, NX), jax.random.fold_in(arg_keys[3], 1), 0, NX - 1).astype(jnp.int32)
    cell_y = with_ends(jax.random.randint(arg_keys[4], (MARKERS,), 0, NY), jax.random.fold_in(arg_keys[4], 1), 0, NY - 1).astype(jnp.int32)
    cell_z = with_ends(jax.random.randint(arg_keys[5], (MARKERS,), 0, BANDZ - 3), jax.random.fold_in(arg_keys[5], 1), 0, (BANDZ - 3) - 1).astype(jnp.int32)
    band_start = draw_band_start(jax.random.fold_in(arg_keys[7], 71), 0)
    return dict(velocity=velocity, forces=forces, offsets=offsets, cell_x=cell_x, cell_y=cell_y, cell_z=cell_z, band_start=band_start)


def delta_weights(fraction):
    root_term = jnp.sqrt(1.0 + 4.0 * fraction - 4.0 * fraction * fraction)
    return jnp.stack([(3.0 - 2.0 * fraction - root_term) / 8.0, (3.0 - 2.0 * fraction + root_term) / 8.0, (1.0 + 2.0 * fraction + root_term) / 8.0, (1.0 + 2.0 * fraction - root_term) / 8.0])

def reference(velocity, forces, offsets, cell_x, cell_y, cell_z, band_start):
    owners = jnp.repeat(band_start, MK_DEV * N_COL)
    z_base = owners * CZ + cell_z
    x_weights = delta_weights(offsets[0])
    y_weights = delta_weights(offsets[1]).T
    z_weights = delta_weights(offsets[2])
    y_rounded = lax.optimization_barrier(y_weights.astype(jnp.bfloat16)).astype(jnp.float32)
    y_index = jnp.stack([(cell_y + corner) % NY for corner in range(4)], axis=1).astype(jnp.int32)
    components = jnp.arange(3, dtype=jnp.int32)
    force_t = forces.T
    field = jnp.zeros((NZ, 3, NX, NY), jnp.float32)
    for z_corner in range(4):
        z_index = ((z_base + z_corner) % NZ).astype(jnp.int32)
        for x_corner in range(4):
            x_index = ((cell_x + x_corner) % NX).astype(jnp.int32)
            scaled = z_weights[z_corner][:, None] * force_t * x_weights[x_corner][:, None]
            scaled = lax.optimization_barrier(scaled.astype(jnp.bfloat16)).astype(jnp.float32)
            values = scaled[:, :, None] * y_rounded[:, None, :]
            field = field.at[z_index[:, None, None], components[None, :, None], x_index[:, None, None], y_index[:, None, :]].add(values)
    neighbours = jnp.roll(velocity, 1, 0) + jnp.roll(velocity, -1, 0)
    neighbours = neighbours + jnp.roll(velocity, 1, 2) + jnp.roll(velocity, -1, 2)
    neighbours = neighbours + jnp.roll(velocity, 1, 3) + jnp.roll(velocity, -1, 3)
    velocity_next = velocity + 0.15 * (neighbours - 6.0 * velocity) + field
    return (field, velocity_next)
```

```python
import functools

import jax
import jax.numpy as jnp
from jax import lax
from jax.experimental import pallas as pl
from jax.experimental.pallas import tpu as pltpu
from jax.sharding import PartitionSpec as P

BAND = 4
CORNERS = 4
VISCOUS = 0.15
LANES = 128
SUBLANES = 8
TILE = 16
MESH = pl.DeviceIdType.MESH


def delta_weights(fraction):
    root_term = jnp.sqrt(1.0 + 4.0 * fraction - 4.0 * fraction * fraction)
    return (
        (3.0 - 2.0 * fraction - root_term) / 8.0,
        (3.0 - 2.0 * fraction + root_term) / 8.0,
        (1.0 + 2.0 * fraction + root_term) / 8.0,
        (1.0 + 2.0 * fraction - root_term) / 8.0,
    )


def pick(distance, weights):
    result = jnp.where(distance == 0, weights[0], 0.0)
    for corner in range(1, CORNERS):
        result = jnp.where(distance == corner, weights[corner], result)
    return result


def wrapped(distance, period):
    if period & (period - 1) == 0:
        return distance & (period - 1)
    distance = jnp.where(distance < 0, distance + period, distance)
    return jnp.where(distance >= period, distance - period, distance)


def kernel(
    sizes,
    forces_hbm,
    offsets_hbm,
    cell_x_hbm,
    cell_y_hbm,
    cell_z_hbm,
    band_hbm,
    velocity_hbm,
    own_ref,
    incoming,
    next_ref,
    raw,
    cells,
    band,
    markers,
    lines,
    total,
    z_halo,
    x_halo,
    velocity_ref,
    load_sems,
    send_sems,
    recv_sems,
):
    gz_count, col_count, slab_depth, half_x, width_y, rows = sizes
    full_x = half_x * col_count
    full_z = slab_depth * gz_count
    gz = lax.axis_index("gz")
    col = lax.axis_index("col")
    place_in_band = lax.rem(gz, BAND)
    low_bit, high_bit = lax.rem(place_in_band, 2), place_in_band // 2
    near = [1 - 2 * low_bit, 2 - 4 * high_bit, 3 - 2 * place_in_band]
    far = [by - BAND + 2 * BAND * bit for by, bit in zip(near, (low_bit, high_bit, high_bit))]
    steps = [near[0], near[1], near[2], far[1], far[0], far[2]]
    starts = [0, 0, 1, 2, 2, 3]
    halo_start = 4

    def gz_at(by):
        return lax.rem(gz + (by + gz_count), gz_count)

    other_col = lax.rem(col + 1, col_count)

    barrier = pltpu.get_barrier_semaphore()
    for by in steps:
        pl.semaphore_signal(barrier, inc=1, device_id={"gz": gz_at(by)}, device_id_type=MESH)
    pl.semaphore_signal(barrier, inc=1, device_id={"col": other_col}, device_id_type=MESH)

    loads = [
        pltpu.make_async_copy(source, target, load_sems.at[index])
        for index, (source, target) in enumerate(
            (
                (forces_hbm, raw.at[0]),
                (offsets_hbm, raw.at[1]),
                (cell_x_hbm, cells.at[0]),
                (cell_y_hbm, cells.at[1]),
                (cell_z_hbm, cells.at[2]),
                (band_hbm, band),
                (velocity_hbm, velocity_ref),
            )
        )
    ]
    for load in loads:
        load.start()
    for load in loads[:-1]:
        load.wait()
    for kind in range(2):
        for c in range(3):
            for row in range(rows):
                place = (3 * kind + c) * rows + row
                markers[0, place : place + 1, :] = raw[kind, c : c + 1, row * LANES : (row + 1) * LANES]
    x_at, y_at, z_at = 6 * rows, 7 * rows, 8 * rows
    markers[0, x_at : x_at + rows, :] = cells[0].astype(jnp.float32)
    markers[0, y_at : y_at + rows, :] = cells[1].astype(jnp.float32)
    z_cell = wrapped(cells[2] + band[0] * slab_depth, full_z)
    markers[0, z_at : z_at + rows, :] = z_cell.astype(jnp.float32)

    pl.semaphore_wait(barrier, len(steps) + 1)

    base = len(steps) + 1

    def remote(source, target, slot, device):
        return pltpu.make_async_remote_copy(
            src_ref=source,
            dst_ref=target,
            send_sem=send_sems.at[slot],
            recv_sem=recv_sems.at[slot],
            device_id=device,
            device_id_type=MESH,
        )

    travels = [
        remote(markers.at[0], markers.at[slot + 1], slot + 1, {"gz": gz_at(by)})
        for slot, by in enumerate(steps)
    ]
    halos = [
        remote(velocity_ref.at[slab_depth - 1], z_halo.at[0], base, {"gz": gz_at(1)}),
        remote(velocity_ref.at[0], z_halo.at[1], base + 1, {"gz": gz_at(-1)}),
        remote(
            velocity_ref.at[:, :, half_x - SUBLANES : half_x],
            x_halo.at[0],
            base + 2,
            {"col": other_col},
        ),
        remote(velocity_ref.at[:, :, 0:SUBLANES], x_halo.at[1], base + 3, {"col": other_col}),
    ]
    exchanges = [
        remote(
            total.at[c * full_x + half_x : (c + 1) * full_x],
            incoming.at[c],
            base + 4 + c,
            {"col": other_col},
        )
        for c in range(3)
    ]
    for travel, start in zip(travels, starts):
        if start == 0:
            travel.start()

    total[...] = jnp.zeros_like(total)

    first_x = col * half_x
    first_z = gz * slab_depth
    sub = lax.broadcasted_iota(jnp.int32, (TILE, LANES), 0)
    zero = jnp.zeros((TILE, LANES), jnp.bfloat16)

    def factors(source):
        def param(index):
            return markers[source, index * rows : (index + 1) * rows, :]

        z_cell = param(8).astype(jnp.int32)
        wz = delta_weights(param(5))
        values = [param(c) for c in range(3)]
        values.extend(delta_weights(param(3)))
        values.extend(w.astype(jnp.bfloat16).astype(jnp.float32) for w in delta_weights(param(4)))
        for plane in range(slab_depth):
            values.append(pick(wrapped(plane + first_z - z_cell, full_z), wz))
        for index, value in enumerate(values):
            lines[index * rows : (index + 1) * rows, :] = value
        x_cell = wrapped(param(6).astype(jnp.int32) - first_x, full_x)
        y_cell = param(7).astype(jnp.int32)
        lefts, rights = [], []
        for row in range(rows):

            def line(index):
                start = index * rows + row
                return jnp.broadcast_to(lines[start : start + 1, :], (TILE, LANES))

            def tiles(cell, first_weight, scales, width):
                at = jnp.broadcast_to(cell[row : row + 1, :], (TILE, LANES))
                past = (sub - at) & (TILE - 1)
                hits = pick(past, [line(first_weight + corner) for corner in range(CORNERS)])
                block = wrapped(at + past, width) // TILE
                block = block.astype(jnp.float32).astype(jnp.bfloat16)
                scaled = [(hits * line(scale)).astype(jnp.bfloat16) for scale in scales]
                members = [block == jnp.asarray(b, jnp.bfloat16) for b in range(width // TILE)]
                return jnp.concatenate(
                    [jnp.where(member, value, zero) for value in scaled for member in members],
                    axis=0,
                )

            lefts.append(tiles(x_cell, 3, range(3), full_x))
            rights.append(tiles(y_cell, 7, range(11, 11 + slab_depth), width_y))
        return jnp.concatenate(lefts, axis=1), jnp.concatenate(rights, axis=1)

    def one_source(source, _):
        for begin in sorted(set(starts) - {0}):

            @pl.when(source == begin)
            def _():
                for travel, start in zip(travels, starts):
                    if start == begin:
                        travel.start()

        @pl.when(source == halo_start)
        def _():
            loads[-1].wait()
            for halo in halos:
                halo.start()

        @pl.when(source > 0)
        def _():
            remote(markers.at[0], markers.at[source], source, {"gz": gz_at(1)}).wait_recv()

        left, right = factors(source)
        total[...] += lax.dot_general(
            left, right, (((1,), (1,)), ((), ())), preferred_element_type=jnp.float32
        )
        return 0

    lax.fori_loop(0, len(steps) + 1, one_source, 0)

    for exchange in exchanges:
        exchange.start()

    for halo in halos:
        halo.wait_recv()
    x_index = lax.broadcasted_iota(jnp.int32, (half_x, width_y), 0)
    for c in range(3):
        own_ref[c] = total[c * full_x : c * full_x + half_x]
    for plane in range(slab_depth):
        for component in range(3):
            here = velocity_ref[plane, component]
            below = z_halo[0, component] if plane == 0 else velocity_ref[plane - 1, component]
            above = (
                z_halo[1, component]
                if plane == slab_depth - 1
                else velocity_ref[plane + 1, component]
            )
            low = x_halo[0, plane, component, SUBLANES - 1 : SUBLANES, :]
            high = x_halo[1, plane, component, 0:1, :]
            x_low = jnp.where(x_index == 0, low, pltpu.roll(here, 1, 0))
            x_high = jnp.where(x_index == half_x - 1, high, pltpu.roll(here, half_x - 1, 0))
            around = above + below + x_low + x_high
            around = around + pltpu.roll(here, 1, 1) + pltpu.roll(here, width_y - 1, 1)
            next_ref[plane, component] = here + VISCOUS * (around - 6.0 * here)

    for exchange in exchanges:
        exchange.wait_recv()
    for copy in travels + halos + exchanges:
        copy.wait_send()


def finish(own_ref, incoming_ref, next_ref, field_hbm, next_hbm, field, after, sems):
    slab_depth, components, _, width_y = field.shape
    copies = []
    for plane in range(slab_depth):
        for c in range(components):
            lanes = slice(plane * width_y, (plane + 1) * width_y)
            value = own_ref[c, :, lanes] + incoming_ref[c, :, lanes]
            field[plane, c] = value
            after[plane, c] = next_ref[plane, c] + value
        for index, (source, target) in enumerate(((field, field_hbm), (after, next_hbm))):
            copy = pltpu.make_async_copy(
                source.at[plane], target.at[plane], sems.at[index, plane]
            )
            copy.start()
            copies.append(copy)
    for copy in copies:
        copy.wait()


def on_device(sizes, velocity, forces, offsets, cell_x, cell_y, cell_z, band_start):
    gz_count, col_count, slab_depth, half_x, width_y, rows = sizes
    full_x = half_x * col_count
    sources = 2 * BAND - 1
    copies = sources + 4 + 3
    shape = jax.ShapeDtypeStruct(velocity.shape, jnp.float32)
    half = jax.ShapeDtypeStruct((3, half_x, slab_depth * width_y), jnp.float32)
    vmem = pl.BlockSpec(memory_space=pltpu.VMEM)
    anywhere = pl.BlockSpec(memory_space=pltpu.HBM)
    own, incoming, after = pl.pallas_call(
        functools.partial(kernel, sizes),
        out_shape=(half, half, shape),
        in_specs=[anywhere] * 7,
        out_specs=(vmem,) * 3,
        scratch_shapes=[
            pltpu.VMEM((2,) + forces.shape, jnp.float32),
            pltpu.VMEM((3, rows, LANES), jnp.int32),
            pltpu.SMEM((1,), jnp.int32),
            pltpu.VMEM((sources, 9 * rows, LANES), jnp.float32),
            pltpu.VMEM(((11 + slab_depth) * rows, LANES), jnp.float32),
            pltpu.VMEM((3 * full_x, slab_depth * width_y), jnp.float32),
            pltpu.VMEM((2,) + velocity.shape[1:], jnp.float32),
            pltpu.VMEM((2, slab_depth, 3, SUBLANES, width_y), jnp.float32),
            pltpu.VMEM(velocity.shape, jnp.float32),
            pltpu.SemaphoreType.DMA((7,)),
            pltpu.SemaphoreType.DMA((copies,)),
            pltpu.SemaphoreType.DMA((copies,)),
        ],
        compiler_params=pltpu.CompilerParams(
            collective_id=0, has_side_effects=True, vmem_limit_bytes=24 * 1024 * 1024
        ),
    )(
        forces,
        offsets,
        cell_x.reshape(rows, LANES),
        cell_y.reshape(rows, LANES),
        cell_z.reshape(rows, LANES),
        band_start,
        velocity,
    )
    return pl.pallas_call(
        finish,
        out_shape=(shape, shape),
        in_specs=[vmem] * 3,
        out_specs=(anywhere,) * 2,
        scratch_shapes=[
            pltpu.VMEM(velocity.shape, jnp.float32),
            pltpu.VMEM(velocity.shape, jnp.float32),
            pltpu.SemaphoreType.DMA((2, slab_depth)),
        ],
        compiler_params=pltpu.CompilerParams(vmem_limit_bytes=16 * 1024 * 1024),
    )(own, incoming, after)


def solution(mesh):
    from_shapes = functools.partial(sized, mesh)
    in_specs = (
        P("gz", None, "col", None),
        P(None, ("gz", "col")),
        P(None, ("gz", "col")),
        P(("gz", "col")),
        P(("gz", "col")),
        P(("gz", "col")),
        P("gz"),
    )
    out_specs = (P("gz", None, "col", None), P("gz", None, "col", None))
    return jax.shard_map(
        from_shapes, mesh=mesh, in_specs=in_specs, out_specs=out_specs, check_vma=False
    )


def sized(mesh, velocity, forces, offsets, cell_x, cell_y, cell_z, band_start):
    slab_depth, _, half_x, width_y = velocity.shape
    rows = cell_x.shape[0] // LANES
    sizes = (mesh.shape["gz"], mesh.shape["col"], slab_depth, half_x, width_y, rows)
    return on_device(sizes, velocity, forces, offsets, cell_x, cell_y, cell_z, band_start)
```

```python
import functools

import jax
import jax.numpy as jnp
from jax import lax
from jax.experimental import pallas as pl
from jax.experimental.pallas import tpu as pltpu
from jax.sharding import PartitionSpec as P

BAND = 4
CORNERS = 4
VISCOUS = 0.15
LANES = 128
SUBLANES = 8
TILE = 16
PIECES = 2 * BAND - 1
MESH = pl.DeviceIdType.MESH


def delta_weights(fraction):
    root_term = jnp.sqrt(1.0 + 4.0 * fraction - 4.0 * fraction * fraction)
    return (
        (3.0 - 2.0 * fraction - root_term) / 8.0,
        (3.0 - 2.0 * fraction + root_term) / 8.0,
        (1.0 + 2.0 * fraction + root_term) / 8.0,
        (1.0 + 2.0 * fraction - root_term) / 8.0,
    )


def pick(distance, weights):
    result = jnp.where(distance == 0, weights[0], 0.0)
    for corner in range(1, CORNERS):
        result = jnp.where(distance == corner, weights[corner], result)
    return result


def wrapped(distance, period):
    if period & (period - 1) == 0:
        return distance & (period - 1)
    distance = jnp.where(distance < 0, distance + period, distance)
    return jnp.where(distance >= period, distance - period, distance)


def kernel(
    sizes,
    forces_hbm,
    offsets_hbm,
    cell_x_hbm,
    cell_y_hbm,
    cell_z_hbm,
    band_hbm,
    velocity_hbm,
    own_ref,
    incoming,
    next_ref,
    raw,
    cells,
    band,
    markers,
    lines,
    total,
    z_halo,
    x_halo,
    velocity_ref,
    load_sems,
    send_sems,
    recv_sems,
):
    gz_count, col_count, slab_depth, half_x, width_y, rows = sizes
    full_x = half_x * col_count
    full_z = slab_depth * gz_count
    gz = lax.axis_index("gz")
    col = lax.axis_index("col")
    place = lax.rem(gz, BAND)
    x_bit, y_bit = lax.rem(place, 2), place // 2
    in_plane = [1 - 2 * x_bit, 2 - 4 * y_bit, 3 - 2 * place]
    onward = [BAND - 2 * BAND * x_bit, BAND - 2 * BAND * y_bit, BAND - 2 * BAND * y_bit]
    peers = in_plane + [BAND, -BAND, 1, -1]
    halo_start = 4

    def gz_at(by):
        return lax.rem(gz + (by + gz_count), gz_count)

    other_col = lax.rem(col + 1, col_count)
    piece = rows // 2

    barrier = pltpu.get_barrier_semaphore()
    for by in peers:
        pl.semaphore_signal(barrier, inc=1, device_id={"gz": gz_at(by)}, device_id_type=MESH)
    pl.semaphore_signal(barrier, inc=1, device_id={"col": other_col}, device_id_type=MESH)

    loads = [
        pltpu.make_async_copy(source, target, load_sems.at[index])
        for index, (source, target) in enumerate(
            (
                (forces_hbm, raw.at[0]),
                (offsets_hbm, raw.at[1]),
                (cell_x_hbm, cells.at[0]),
                (cell_y_hbm, cells.at[1]),
                (cell_z_hbm, cells.at[2]),
                (band_hbm, band),
                (velocity_hbm, velocity_ref),
            )
        )
    ]
    for load in loads:
        load.start()
    for load in loads[:-1]:
        load.wait()
    for kind in range(2):
        for c in range(3):
            for row in range(rows):
                at = (3 * kind + c) * piece + row % piece
                lanes = slice(row * LANES, (row + 1) * LANES)
                markers[row // piece, at : at + 1, :] = raw[kind, c : c + 1, lanes]
    z_cell = wrapped(cells[2] + band[0] * slab_depth, full_z)
    for index, value in ((6, cells[0]), (7, cells[1]), (8, z_cell)):
        for h in range(2):
            at = index * piece
            markers[h, at : at + piece, :] = value[h * piece : (h + 1) * piece].astype(jnp.float32)

    pl.semaphore_wait(barrier, len(peers) + 1)

    base = 2 * PIECES

    def remote(source, target, slot, device):
        return pltpu.make_async_remote_copy(
            src_ref=source,
            dst_ref=target,
            send_sem=send_sems.at[slot],
            recv_sem=recv_sems.at[slot],
            device_id=device,
            device_id_type=MESH,
        )

    def travel(source, target, by):
        return remote(markers.at[source], markers.at[target], target, {"gz": gz_at(by)})

    way = [0, 1, 0, 1, 2, 2]
    firsts = [travel(t // 2 if t < 4 else t - 4, t + 2, in_plane[way[t]]) for t in range(6)]
    seconds = [travel(t + 2, t + 8, onward[way[t]]) for t in range(6)]
    halos = [
        remote(velocity_ref.at[slab_depth - 1], z_halo.at[0], base, {"gz": gz_at(1)}),
        remote(velocity_ref.at[0], z_halo.at[1], base + 1, {"gz": gz_at(-1)}),
        remote(
            velocity_ref.at[:, :, half_x - SUBLANES : half_x],
            x_halo.at[0],
            base + 2,
            {"col": other_col},
        ),
        remote(velocity_ref.at[:, :, 0:SUBLANES], x_halo.at[1], base + 3, {"col": other_col}),
    ]
    exchanges = [
        remote(
            total.at[c * full_x + half_x : (c + 1) * full_x],
            incoming.at[c],
            base + 4 + c,
            {"col": other_col},
        )
        for c in range(3)
    ]
    for copy in firsts[:4]:
        copy.start()

    total[...] = jnp.zeros_like(total)

    first_x = col * half_x
    first_z = gz * slab_depth
    sub = lax.broadcasted_iota(jnp.int32, (TILE, LANES), 0)
    zero = jnp.zeros((TILE, LANES), jnp.bfloat16)

    def factors(turn):
        def param(index):
            at = index * piece
            return jnp.concatenate(
                [markers[2 * turn + h, at : at + piece, :] for h in range(2)], axis=0
            )

        z_cell = param(8).astype(jnp.int32)
        wz = delta_weights(param(5))
        values = [param(c) for c in range(3)]
        values.extend(delta_weights(param(3)))
        values.extend(w.astype(jnp.bfloat16).astype(jnp.float32) for w in delta_weights(param(4)))
        for plane in range(slab_depth):
            values.append(pick(wrapped(plane + first_z - z_cell, full_z), wz))
        for index, value in enumerate(values):
            lines[index * rows : (index + 1) * rows, :] = value
        x_cell = wrapped(param(6).astype(jnp.int32) - first_x, full_x)
        y_cell = param(7).astype(jnp.int32)
        lefts, rights = [], []
        for row in range(rows):

            def line(index):
                start = index * rows + row
                return jnp.broadcast_to(lines[start : start + 1, :], (TILE, LANES))

            def tiles(cell, first_weight, scales, width):
                at = jnp.broadcast_to(cell[row : row + 1, :], (TILE, LANES))
                past = (sub - at) & (TILE - 1)
                hits = pick(past, [line(first_weight + corner) for corner in range(CORNERS)])
                block = wrapped(at + past, width) // TILE
                block = block.astype(jnp.float32).astype(jnp.bfloat16)
                scaled = [(hits * line(scale)).astype(jnp.bfloat16) for scale in scales]
                members = [block == jnp.asarray(b, jnp.bfloat16) for b in range(width // TILE)]
                return jnp.concatenate(
                    [jnp.where(member, value, zero) for value in scaled for member in members],
                    axis=0,
                )

            lefts.append(tiles(x_cell, 3, range(3), full_x))
            rights.append(tiles(y_cell, 7, range(11, 11 + slab_depth), width_y))
        return jnp.concatenate(lefts, axis=1), jnp.concatenate(rights, axis=1)

    def one_turn(turn, _):
        @pl.when(turn > 0)
        def _():
            for h in range(2):
                travel(0, 2 * turn + h, 1).wait_recv()

        @pl.when(turn == 1)
        def _():
            for copy in firsts[4:]:
                copy.start()

        for step in range(3):

            @pl.when(turn == step + 1)
            def _():
                for copy in seconds[2 * step : 2 * step + 2]:
                    copy.start()

        @pl.when(turn == halo_start)
        def _():
            loads[-1].wait()
            for halo in halos:
                halo.start()

        left, right = factors(turn)
        total[...] += lax.dot_general(
            left, right, (((1,), (1,)), ((), ())), preferred_element_type=jnp.float32
        )
        return 0

    lax.fori_loop(0, PIECES, one_turn, 0)

    for exchange in exchanges:
        exchange.start()

    for halo in halos:
        halo.wait_recv()
    x_index = lax.broadcasted_iota(jnp.int32, (half_x, width_y), 0)
    for c in range(3):
        own_ref[c] = total[c * full_x : c * full_x + half_x]
    for plane in range(slab_depth):
        for component in range(3):
            here = velocity_ref[plane, component]
            below = z_halo[0, component] if plane == 0 else velocity_ref[plane - 1, component]
            above = (
                z_halo[1, component]
                if plane == slab_depth - 1
                else velocity_ref[plane + 1, component]
            )
            low = x_halo[0, plane, component, SUBLANES - 1 : SUBLANES, :]
            high = x_halo[1, plane, component, 0:1, :]
            x_low = jnp.where(x_index == 0, low, pltpu.roll(here, 1, 0))
            x_high = jnp.where(x_index == half_x - 1, high, pltpu.roll(here, half_x - 1, 0))
            around = above + below + x_low + x_high
            around = around + pltpu.roll(here, 1, 1) + pltpu.roll(here, width_y - 1, 1)
            next_ref[plane, component] = here + VISCOUS * (around - 6.0 * here)

    for exchange in exchanges:
        exchange.wait_recv()
    for copy in firsts + seconds + halos + exchanges:
        copy.wait_send()


def finish(own_ref, incoming_ref, next_ref, field_hbm, next_hbm, field, after, sems):
    slab_depth, components, _, width_y = field.shape
    copies = []
    for plane in range(slab_depth):
        for c in range(components):
            lanes = slice(plane * width_y, (plane + 1) * width_y)
            value = own_ref[c, :, lanes] + incoming_ref[c, :, lanes]
            field[plane, c] = value
            after[plane, c] = next_ref[plane, c] + value
        for index, (source, target) in enumerate(((field, field_hbm), (after, next_hbm))):
            copy = pltpu.make_async_copy(
                source.at[plane], target.at[plane], sems.at[index, plane]
            )
            copy.start()
            copies.append(copy)
    for copy in copies:
        copy.wait()


def on_device(sizes, velocity, forces, offsets, cell_x, cell_y, cell_z, band_start):
    gz_count, col_count, slab_depth, half_x, width_y, rows = sizes
    full_x = half_x * col_count
    copies = 2 * PIECES + 4 + 3
    shape = jax.ShapeDtypeStruct(velocity.shape, jnp.float32)
    half = (3, half_x, slab_depth * width_y)
    vmem = pl.BlockSpec(memory_space=pltpu.VMEM)
    anywhere = pl.BlockSpec(memory_space=pltpu.HBM)
    own, incoming, after = pl.pallas_call(
        functools.partial(kernel, sizes),
        out_shape=(pltpu.VMEM(half, jnp.float32), pltpu.VMEM(half, jnp.float32), pltpu.VMEM(velocity.shape, jnp.float32)),
        in_specs=[anywhere] * 7,
        out_specs=(vmem,) * 3,
        scratch_shapes=[
            pltpu.VMEM((2,) + forces.shape, jnp.float32),
            pltpu.VMEM((3, rows, LANES), jnp.int32),
            pltpu.SMEM((1,), jnp.int32),
            pltpu.VMEM((2 * PIECES, 9 * rows // 2, LANES), jnp.float32),
            pltpu.VMEM(((11 + slab_depth) * rows, LANES), jnp.float32),
            pltpu.VMEM((3 * full_x, slab_depth * width_y), jnp.float32),
            pltpu.VMEM((2,) + velocity.shape[1:], jnp.float32),
            pltpu.VMEM((2, slab_depth, 3, SUBLANES, width_y), jnp.float32),
            pltpu.VMEM(velocity.shape, jnp.float32),
            pltpu.SemaphoreType.DMA((7,)),
            pltpu.SemaphoreType.DMA((copies,)),
            pltpu.SemaphoreType.DMA((copies,)),
        ],
        compiler_params=pltpu.CompilerParams(
            collective_id=0, has_side_effects=True, vmem_limit_bytes=56 * 1024 * 1024
        ),
    )(
        forces,
        offsets,
        cell_x.reshape(rows, LANES),
        cell_y.reshape(rows, LANES),
        cell_z.reshape(rows, LANES),
        band_start,
        velocity,
    )
    return pl.pallas_call(
        finish,
        out_shape=(shape, shape),
        in_specs=[vmem] * 3,
        out_specs=(anywhere,) * 2,
        scratch_shapes=[
            pltpu.VMEM(velocity.shape, jnp.float32),
            pltpu.VMEM(velocity.shape, jnp.float32),
            pltpu.SemaphoreType.DMA((2, slab_depth)),
        ],
        compiler_params=pltpu.CompilerParams(vmem_limit_bytes=16 * 1024 * 1024),
    )(own, incoming, after)


def solution(mesh):
    from_shapes = functools.partial(sized, mesh)
    in_specs = (
        P("gz", None, "col", None),
        P(None, ("gz", "col")),
        P(None, ("gz", "col")),
        P(("gz", "col")),
        P(("gz", "col")),
        P(("gz", "col")),
        P("gz"),
    )
    out_specs = (P("gz", None, "col", None), P("gz", None, "col", None))
    return jax.shard_map(
        from_shapes, mesh=mesh, in_specs=in_specs, out_specs=out_specs, check_vma=False
    )


def sized(mesh, velocity, forces, offsets, cell_x, cell_y, cell_z, band_start):
    slab_depth, _, half_x, width_y = velocity.shape
    rows = cell_x.shape[0] // LANES
    sizes = (mesh.shape["gz"], mesh.shape["col"], slab_depth, half_x, width_y, rows)
    return on_device(sizes, velocity, forces, offsets, cell_x, cell_y, cell_z, band_start)
```

```python
import functools

import jax
import jax.numpy as jnp
from jax import lax
from jax.experimental import pallas as pl
from jax.experimental.pallas import tpu as pltpu
from jax.sharding import PartitionSpec as P

BAND = 4
CORNERS = 4
VISCOUS = 0.15
LANES = 128
SUBLANES = 8
TILE = 16
PIECES = 2 * BAND - 1
MESH = pl.DeviceIdType.MESH


def delta_weights(fraction):
    root_term = jnp.sqrt(1.0 + 4.0 * fraction - 4.0 * fraction * fraction)
    return (
        (3.0 - 2.0 * fraction - root_term) / 8.0,
        (3.0 - 2.0 * fraction + root_term) / 8.0,
        (1.0 + 2.0 * fraction + root_term) / 8.0,
        (1.0 + 2.0 * fraction - root_term) / 8.0,
    )


def pick(distance, weights):
    result = jnp.where(distance == 0, weights[0], 0.0)
    for corner in range(1, CORNERS):
        result = jnp.where(distance == corner, weights[corner], result)
    return result


def wrapped(distance, period):
    if period & (period - 1) == 0:
        return distance & (period - 1)
    distance = jnp.where(distance < 0, distance + period, distance)
    return jnp.where(distance >= period, distance - period, distance)


def kernel(
    sizes,
    forces_hbm,
    offsets_hbm,
    cell_x_hbm,
    cell_y_hbm,
    cell_z_hbm,
    band_hbm,
    velocity_hbm,
    own_ref,
    incoming,
    next_ref,
    raw,
    cells,
    band,
    markers,
    lines,
    total,
    z_halo,
    x_halo,
    velocity_ref,
    load_sems,
    send_sems,
    recv_sems,
):
    gz_count, col_count, slab_depth, half_x, width_y, rows = sizes
    full_x = half_x * col_count
    full_z = slab_depth * gz_count
    gz = lax.axis_index("gz")
    col = lax.axis_index("col")
    place = lax.rem(gz, BAND)
    x_bit, y_bit = lax.rem(place, 2), place // 2
    in_plane = [1 - 2 * x_bit, 2 - 4 * y_bit, 3 - 2 * place]
    onward = [BAND - 2 * BAND * x_bit, BAND - 2 * BAND * y_bit, BAND - 2 * BAND * y_bit]
    peers = in_plane + [BAND, -BAND, 1, -1]
    halo_start = 4

    def gz_at(by):
        return lax.rem(gz + (by + gz_count), gz_count)

    other_col = lax.rem(col + 1, col_count)
    piece = rows // 2

    barrier = pltpu.get_barrier_semaphore()
    for by in peers:
        pl.semaphore_signal(barrier, inc=1, device_id={"gz": gz_at(by)}, device_id_type=MESH)
    pl.semaphore_signal(barrier, inc=1, device_id={"col": other_col}, device_id_type=MESH)

    loads = [
        pltpu.make_async_copy(source, target, load_sems.at[index])
        for index, (source, target) in enumerate(
            (
                (forces_hbm, raw.at[0]),
                (offsets_hbm, raw.at[1]),
                (cell_x_hbm, cells.at[0]),
                (cell_y_hbm, cells.at[1]),
                (cell_z_hbm, cells.at[2]),
                (band_hbm, band),
                (velocity_hbm, velocity_ref),
            )
        )
    ]
    for load in loads:
        load.start()
    for load in loads[:-1]:
        load.wait()
    z_cell = wrapped(cells[2] + band[0] * slab_depth, full_z)

    def assemble(h):
        for kind in range(2):
            for c in range(3):
                for row in range(h * piece, (h + 1) * piece):
                    at = (3 * kind + c) * piece + row % piece
                    lanes = slice(row * LANES, (row + 1) * LANES)
                    markers[h, at : at + 1, :] = raw[kind, c : c + 1, lanes]
        for index, value in ((6, cells[0]), (7, cells[1]), (8, z_cell)):
            at = index * piece
            markers[h, at : at + piece, :] = value[h * piece : (h + 1) * piece].astype(jnp.float32)

    assemble(0)
    pl.semaphore_wait(barrier, len(peers) + 1)

    base = 2 * PIECES

    def remote(source, target, slot, device):
        return pltpu.make_async_remote_copy(
            src_ref=source,
            dst_ref=target,
            send_sem=send_sems.at[slot],
            recv_sem=recv_sems.at[slot],
            device_id=device,
            device_id_type=MESH,
        )

    def travel(source, target, by):
        return remote(markers.at[source], markers.at[target], target, {"gz": gz_at(by)})

    way = [0, 1, 0, 1, 2, 2]
    firsts = [travel(t // 2 if t < 4 else t - 4, t + 2, in_plane[way[t]]) for t in range(6)]
    seconds = [travel(t + 2, t + 8, onward[way[t]]) for t in range(6)]
    halos = [
        remote(velocity_ref.at[slab_depth - 1], z_halo.at[0], base, {"gz": gz_at(1)}),
        remote(velocity_ref.at[0], z_halo.at[1], base + 1, {"gz": gz_at(-1)}),
        remote(
            velocity_ref.at[:, :, half_x - SUBLANES : half_x],
            x_halo.at[0],
            base + 2,
            {"col": other_col},
        ),
        remote(velocity_ref.at[:, :, 0:SUBLANES], x_halo.at[1], base + 3, {"col": other_col}),
    ]
    exchanges = [
        remote(
            total.at[c * full_x + half_x : (c + 1) * full_x],
            incoming.at[c],
            base + 4 + c,
            {"col": other_col},
        )
        for c in range(3)
    ]
    for copy in firsts[:2]:
        copy.start()
    assemble(1)
    for copy in firsts[2:4]:
        copy.start()

    total[...] = jnp.zeros_like(total)

    first_x = col * half_x
    first_z = gz * slab_depth
    sub = lax.broadcasted_iota(jnp.int32, (TILE, LANES), 0)
    zero = jnp.zeros((TILE, LANES), jnp.bfloat16)

    def factors(turn):
        def param(index):
            at = index * piece
            return jnp.concatenate(
                [markers[2 * turn + h, at : at + piece, :] for h in range(2)], axis=0
            )

        z_cell = param(8).astype(jnp.int32)
        wz = delta_weights(param(5))
        values = [param(c) for c in range(3)]
        values.extend(delta_weights(param(3)))
        values.extend(w.astype(jnp.bfloat16).astype(jnp.float32) for w in delta_weights(param(4)))
        for plane in range(slab_depth):
            values.append(pick(wrapped(plane + first_z - z_cell, full_z), wz))
        for index, value in enumerate(values):
            lines[index * rows : (index + 1) * rows, :] = value
        x_cell = wrapped(param(6).astype(jnp.int32) - first_x, full_x)
        y_cell = param(7).astype(jnp.int32)
        lefts, rights = [], []
        for row in range(rows):

            def line(index):
                start = index * rows + row
                return jnp.broadcast_to(lines[start : start + 1, :], (TILE, LANES))

            def tiles(cell, first_weight, scales, width):
                at = jnp.broadcast_to(cell[row : row + 1, :], (TILE, LANES))
                past = (sub - at) & (TILE - 1)
                hits = pick(past, [line(first_weight + corner) for corner in range(CORNERS)])
                block = wrapped(at + past, width) // TILE
                block = block.astype(jnp.float32).astype(jnp.bfloat16)
                scaled = [(hits * line(scale)).astype(jnp.bfloat16) for scale in scales]
                members = [block == jnp.asarray(b, jnp.bfloat16) for b in range(width // TILE)]
                return jnp.concatenate(
                    [jnp.where(member, value, zero) for value in scaled for member in members],
                    axis=0,
                )

            lefts.append(tiles(x_cell, 3, range(3), full_x))
            rights.append(tiles(y_cell, 7, range(11, 11 + slab_depth), width_y))
        return jnp.concatenate(lefts, axis=1), jnp.concatenate(rights, axis=1)

    def one_turn(turn, _):
        @pl.when(turn > 0)
        def _():
            for h in range(2):
                travel(0, 2 * turn + h, 1).wait_recv()

        @pl.when(turn == 1)
        def _():
            for copy in firsts[4:]:
                copy.start()

        for step in range(3):

            @pl.when(turn == step + 1)
            def _():
                for copy in seconds[2 * step : 2 * step + 2]:
                    copy.start()

        @pl.when(turn == halo_start)
        def _():
            loads[-1].wait()
            for halo in halos:
                halo.start()

        left, right = factors(turn)
        total[...] += lax.dot_general(
            left, right, (((1,), (1,)), ((), ())), preferred_element_type=jnp.float32
        )
        return 0

    lax.fori_loop(0, PIECES, one_turn, 0)

    for exchange in exchanges:
        exchange.start()

    for halo in halos:
        halo.wait_recv()
    x_index = lax.broadcasted_iota(jnp.int32, (half_x, width_y), 0)
    for c in range(3):
        own_ref[c] = total[c * full_x : c * full_x + half_x]
    for plane in range(slab_depth):
        for component in range(3):
            here = velocity_ref[plane, component]
            below = z_halo[0, component] if plane == 0 else velocity_ref[plane - 1, component]
            above = (
                z_halo[1, component]
                if plane == slab_depth - 1
                else velocity_ref[plane + 1, component]
            )
            low = x_halo[0, plane, component, SUBLANES - 1 : SUBLANES, :]
            high = x_halo[1, plane, component, 0:1, :]
            x_low = jnp.where(x_index == 0, low, pltpu.roll(here, 1, 0))
            x_high = jnp.where(x_index == half_x - 1, high, pltpu.roll(here, half_x - 1, 0))
            around = above + below + x_low + x_high
            around = around + pltpu.roll(here, 1, 1) + pltpu.roll(here, width_y - 1, 1)
            lanes = slice(plane * width_y, (plane + 1) * width_y)
            rest = here + VISCOUS * (around - 6.0 * here)
            next_ref[plane, component] = rest + own_ref[component, :, lanes]

    for exchange in exchanges:
        exchange.wait_recv()
    for copy in firsts + seconds + halos + exchanges:
        copy.wait_send()


def finish(own_ref, incoming_ref, next_ref, field_hbm, next_hbm, field, after, sems):
    slab_depth, components, _, width_y = field.shape
    copies = []
    for plane in range(slab_depth):
        for c in range(components):
            lanes = slice(plane * width_y, (plane + 1) * width_y)
            value = incoming_ref[c, :, lanes]
            field[plane, c] = own_ref[c, :, lanes] + value
            after[plane, c] = next_ref[plane, c] + value
        for index, (source, target) in enumerate(((field, field_hbm), (after, next_hbm))):
            copy = pltpu.make_async_copy(
                source.at[plane], target.at[plane], sems.at[index, plane]
            )
            copy.start()
            copies.append(copy)
    for copy in copies:
        copy.wait()


def on_device(sizes, velocity, forces, offsets, cell_x, cell_y, cell_z, band_start):
    gz_count, col_count, slab_depth, half_x, width_y, rows = sizes
    full_x = half_x * col_count
    copies = 2 * PIECES + 4 + 3
    shape = jax.ShapeDtypeStruct(velocity.shape, jnp.float32)
    half = (3, half_x, slab_depth * width_y)
    vmem = pl.BlockSpec(memory_space=pltpu.VMEM)
    anywhere = pl.BlockSpec(memory_space=pltpu.HBM)
    own, incoming, after = pl.pallas_call(
        functools.partial(kernel, sizes),
        out_shape=(pltpu.VMEM(half, jnp.float32), pltpu.VMEM(half, jnp.float32), pltpu.VMEM(velocity.shape, jnp.float32)),
        in_specs=[anywhere] * 7,
        out_specs=(vmem,) * 3,
        scratch_shapes=[
            pltpu.VMEM((2,) + forces.shape, jnp.float32),
            pltpu.VMEM((3, rows, LANES), jnp.int32),
            pltpu.SMEM((1,), jnp.int32),
            pltpu.VMEM((2 * PIECES, 9 * rows // 2, LANES), jnp.float32),
            pltpu.VMEM(((11 + slab_depth) * rows, LANES), jnp.float32),
            pltpu.VMEM((3 * full_x, slab_depth * width_y), jnp.float32),
            pltpu.VMEM((2,) + velocity.shape[1:], jnp.float32),
            pltpu.VMEM((2, slab_depth, 3, SUBLANES, width_y), jnp.float32),
            pltpu.VMEM(velocity.shape, jnp.float32),
            pltpu.SemaphoreType.DMA((7,)),
            pltpu.SemaphoreType.DMA((copies,)),
            pltpu.SemaphoreType.DMA((copies,)),
        ],
        compiler_params=pltpu.CompilerParams(
            collective_id=0, has_side_effects=True, vmem_limit_bytes=56 * 1024 * 1024
        ),
    )(
        forces,
        offsets,
        cell_x.reshape(rows, LANES),
        cell_y.reshape(rows, LANES),
        cell_z.reshape(rows, LANES),
        band_start,
        velocity,
    )
    return pl.pallas_call(
        finish,
        out_shape=(shape, shape),
        in_specs=[vmem] * 3,
        out_specs=(anywhere,) * 2,
        scratch_shapes=[
            pltpu.VMEM(velocity.shape, jnp.float32),
            pltpu.VMEM(velocity.shape, jnp.float32),
            pltpu.SemaphoreType.DMA((2, slab_depth)),
        ],
        compiler_params=pltpu.CompilerParams(vmem_limit_bytes=16 * 1024 * 1024),
    )(own, incoming, after)


def solution(mesh):
    from_shapes = functools.partial(sized, mesh)
    in_specs = (
        P("gz", None, "col", None),
        P(None, ("gz", "col")),
        P(None, ("gz", "col")),
        P(("gz", "col")),
        P(("gz", "col")),
        P(("gz", "col")),
        P("gz"),
    )
    out_specs = (P("gz", None, "col", None), P("gz", None, "col", None))
    return jax.shard_map(
        from_shapes, mesh=mesh, in_specs=in_specs, out_specs=out_specs, check_vma=False
    )


def sized(mesh, velocity, forces, offsets, cell_x, cell_y, cell_z, band_start):
    slab_depth, _, half_x, width_y = velocity.shape
    rows = cell_x.shape[0] // LANES
    sizes = (mesh.shape["gz"], mesh.shape["col"], slab_depth, half_x, width_y, rows)
    return on_device(sizes, velocity, forces, offsets, cell_x, cell_y, cell_z, band_start)
```

```python
import functools

import jax
import jax.numpy as jnp
from jax import lax
from jax.experimental import pallas as pl
from jax.experimental.pallas import tpu as pltpu
from jax.sharding import PartitionSpec as P

BAND = 4
CORNERS = 4
VISCOUS = 0.15
LANES = 128
SUBLANES = 8
TILE = 16
PIECES = 2 * BAND - 1
MESH = pl.DeviceIdType.MESH


def delta_weights(fraction):
    root_term = jnp.sqrt(1.0 + 4.0 * fraction - 4.0 * fraction * fraction)
    return (
        (3.0 - 2.0 * fraction - root_term) / 8.0,
        (3.0 - 2.0 * fraction + root_term) / 8.0,
        (1.0 + 2.0 * fraction + root_term) / 8.0,
        (1.0 + 2.0 * fraction - root_term) / 8.0,
    )


def pick(distance, weights):
    result = jnp.where(distance == 0, weights[0], 0.0)
    for corner in range(1, CORNERS):
        result = jnp.where(distance == corner, weights[corner], result)
    return result


def wrapped(distance, period):
    if period & (period - 1) == 0:
        return distance & (period - 1)
    distance = jnp.where(distance < 0, distance + period, distance)
    return jnp.where(distance >= period, distance - period, distance)


def kernel(
    sizes,
    forces_hbm,
    offsets_hbm,
    cell_x_hbm,
    cell_y_hbm,
    cell_z_hbm,
    band_hbm,
    velocity_hbm,
    own_ref,
    incoming,
    next_ref,
    raw,
    cells,
    band,
    markers,
    lines,
    total,
    z_halo,
    x_halo,
    velocity_ref,
    load_sems,
    send_sems,
    recv_sems,
):
    gz_count, col_count, slab_depth, half_x, width_y, rows = sizes
    full_x = half_x * col_count
    full_z = slab_depth * gz_count
    gz = lax.axis_index("gz")
    col = lax.axis_index("col")
    place = lax.rem(gz, BAND)
    x_bit, y_bit = lax.rem(place, 2), place // 2
    in_plane = [1 - 2 * x_bit, 2 - 4 * y_bit, 3 - 2 * place]
    onward = [BAND - 2 * BAND * x_bit, BAND - 2 * BAND * y_bit, BAND - 2 * BAND * y_bit]
    peers = in_plane + [BAND, -BAND, 1, -1]
    halo_start = 4

    def gz_at(by):
        return lax.rem(gz + (by + gz_count), gz_count)

    other_col = lax.rem(col + 1, col_count)
    piece = rows // 2

    barrier = pltpu.get_barrier_semaphore()
    for by in peers:
        pl.semaphore_signal(barrier, inc=1, device_id={"gz": gz_at(by)}, device_id_type=MESH)
    pl.semaphore_signal(barrier, inc=1, device_id={"col": other_col}, device_id_type=MESH)

    loads = [
        pltpu.make_async_copy(source, target, load_sems.at[index])
        for index, (source, target) in enumerate(
            (
                (forces_hbm, raw.at[0]),
                (offsets_hbm, raw.at[1]),
                (cell_x_hbm, cells.at[0]),
                (cell_y_hbm, cells.at[1]),
                (cell_z_hbm, cells.at[2]),
                (band_hbm, band),
                (velocity_hbm, velocity_ref),
            )
        )
    ]
    for load in loads:
        load.start()
    for load in loads[:-1]:
        load.wait()
    z_cell = wrapped(cells[2] + band[0] * slab_depth, full_z)

    def assemble(h):
        for kind in range(2):
            for c in range(3):
                for row in range(h * piece, (h + 1) * piece):
                    at = (3 * kind + c) * piece + row % piece
                    lanes = slice(row * LANES, (row + 1) * LANES)
                    markers[h, at : at + 1, :] = raw[kind, c : c + 1, lanes]
        for index, value in ((6, cells[0]), (7, cells[1]), (8, z_cell)):
            at = index * piece
            markers[h, at : at + piece, :] = value[h * piece : (h + 1) * piece].astype(jnp.float32)

    assemble(0)
    pl.semaphore_wait(barrier, len(peers) + 1)

    base = 2 * PIECES

    def remote(source, target, slot, device):
        return pltpu.make_async_remote_copy(
            src_ref=source,
            dst_ref=target,
            send_sem=send_sems.at[slot],
            recv_sem=recv_sems.at[slot],
            device_id=device,
            device_id_type=MESH,
        )

    def travel(source, target, by):
        return remote(markers.at[source], markers.at[target], target, {"gz": gz_at(by)})

    def travel_pair(source, target, by):
        pair = markers.at[pl.ds(target, 2)]
        return remote(markers.at[pl.ds(source, 2)], pair, target, {"gz": gz_at(by)})

    way = [0, 1, 0, 1]
    firsts = [travel(t // 2, t + 2, in_plane[way[t]]) for t in range(4)]
    firsts.append(travel_pair(0, 6, in_plane[2]))
    seconds = [travel(t + 2, t + 8, onward[way[t]]) for t in range(4)]
    seconds.append(travel_pair(6, 12, onward[2]))
    halos = [
        remote(velocity_ref.at[slab_depth - 1], z_halo.at[0], base, {"gz": gz_at(1)}),
        remote(velocity_ref.at[0], z_halo.at[1], base + 1, {"gz": gz_at(-1)}),
        remote(
            velocity_ref.at[:, :, half_x - SUBLANES : half_x],
            x_halo.at[0],
            base + 2,
            {"col": other_col},
        ),
        remote(velocity_ref.at[:, :, 0:SUBLANES], x_halo.at[1], base + 3, {"col": other_col}),
    ]
    exchanges = [
        remote(
            total.at[c * full_x + half_x : (c + 1) * full_x],
            incoming.at[c],
            base + 4 + c,
            {"col": other_col},
        )
        for c in range(3)
    ]
    for copy in firsts[:2]:
        copy.start()
    assemble(1)
    for copy in firsts[2:4]:
        copy.start()

    total[...] = jnp.zeros_like(total)

    first_x = col * half_x
    first_z = gz * slab_depth
    sub = lax.broadcasted_iota(jnp.int32, (TILE, LANES), 0)
    zero = jnp.zeros((TILE, LANES), jnp.bfloat16)

    def factors(turn):
        def param(index):
            at = index * piece
            return jnp.concatenate(
                [markers[2 * turn + h, at : at + piece, :] for h in range(2)], axis=0
            )

        z_cell = param(8).astype(jnp.int32)
        wz = delta_weights(param(5))
        values = [param(c) for c in range(3)]
        values.extend(delta_weights(param(3)))
        values.extend(w.astype(jnp.bfloat16).astype(jnp.float32) for w in delta_weights(param(4)))
        for plane in range(slab_depth):
            values.append(pick(wrapped(plane + first_z - z_cell, full_z), wz))
        for index, value in enumerate(values):
            lines[index * rows : (index + 1) * rows, :] = value
        x_cell = wrapped(param(6).astype(jnp.int32) - first_x, full_x)
        y_cell = param(7).astype(jnp.int32)
        lefts, rights = [], []
        for row in range(rows):

            def line(index):
                start = index * rows + row
                return jnp.broadcast_to(lines[start : start + 1, :], (TILE, LANES))

            def tiles(cell, first_weight, scales, width):
                at = jnp.broadcast_to(cell[row : row + 1, :], (TILE, LANES))
                past = (sub - at) & (TILE - 1)
                hits = pick(past, [line(first_weight + corner) for corner in range(CORNERS)])
                block = wrapped(at + past, width) // TILE
                block = block.astype(jnp.float32).astype(jnp.bfloat16)
                scaled = [(hits * line(scale)).astype(jnp.bfloat16) for scale in scales]
                members = [block == jnp.asarray(b, jnp.bfloat16) for b in range(width // TILE)]
                return jnp.concatenate(
                    [jnp.where(member, value, zero) for value in scaled for member in members],
                    axis=0,
                )

            lefts.append(tiles(x_cell, 3, range(3), full_x))
            rights.append(tiles(y_cell, 7, range(11, 11 + slab_depth), width_y))
        return jnp.concatenate(lefts, axis=1), jnp.concatenate(rights, axis=1)

    def one_turn(turn, _):
        alone = (turn == 3) | (turn == PIECES - 1)

        @pl.when((turn > 0) & jnp.logical_not(alone))
        def _():
            for h in range(2):
                travel(0, 2 * turn + h, 1).wait_recv()

        @pl.when(alone)
        def _():
            travel_pair(0, 2 * turn, 1).wait_recv()

        @pl.when(turn == 1)
        def _():
            for copy in firsts[4:]:
                copy.start()

        for step in range(3):

            @pl.when(turn == step + 1)
            def _():
                for copy in seconds[2 * step : 2 * step + 2]:
                    copy.start()

        @pl.when(turn == halo_start)
        def _():
            loads[-1].wait()
            for halo in halos:
                halo.start()

        left, right = factors(turn)
        total[...] += lax.dot_general(
            left, right, (((1,), (1,)), ((), ())), preferred_element_type=jnp.float32
        )
        return 0

    lax.fori_loop(0, PIECES, one_turn, 0)

    for exchange in exchanges:
        exchange.start()

    for halo in halos:
        halo.wait_recv()
    x_index = lax.broadcasted_iota(jnp.int32, (half_x, width_y), 0)
    for c in range(3):
        own_ref[c] = total[c * full_x : c * full_x + half_x]
    for plane in range(slab_depth):
        for component in range(3):
            here = velocity_ref[plane, component]
            below = z_halo[0, component] if plane == 0 else velocity_ref[plane - 1, component]
            above = (
                z_halo[1, component]
                if plane == slab_depth - 1
                else velocity_ref[plane + 1, component]
            )
            low = x_halo[0, plane, component, SUBLANES - 1 : SUBLANES, :]
            high = x_halo[1, plane, component, 0:1, :]
            x_low = jnp.where(x_index == 0, low, pltpu.roll(here, 1, 0))
            x_high = jnp.where(x_index == half_x - 1, high, pltpu.roll(here, half_x - 1, 0))
            around = above + below + x_low + x_high
            around = around + pltpu.roll(here, 1, 1) + pltpu.roll(here, width_y - 1, 1)
            lanes = slice(plane * width_y, (plane + 1) * width_y)
            rest = here + VISCOUS * (around - 6.0 * here)
            next_ref[plane, component] = rest + own_ref[component, :, lanes]

    for exchange in exchanges:
        exchange.wait_recv()
    for copy in firsts + seconds + halos + exchanges:
        copy.wait_send()


def finish(own_ref, incoming_ref, next_ref, field_hbm, next_hbm, field, after, sems):
    slab_depth, components, _, width_y = field.shape
    copies = []
    for plane in range(slab_depth):
        for c in range(components):
            lanes = slice(plane * width_y, (plane + 1) * width_y)
            value = incoming_ref[c, :, lanes]
            field[plane, c] = own_ref[c, :, lanes] + value
            after[plane, c] = next_ref[plane, c] + value
        for index, (source, target) in enumerate(((field, field_hbm), (after, next_hbm))):
            copy = pltpu.make_async_copy(
                source.at[plane], target.at[plane], sems.at[index, plane]
            )
            copy.start()
            copies.append(copy)
    for copy in copies:
        copy.wait()


def on_device(sizes, velocity, forces, offsets, cell_x, cell_y, cell_z, band_start):
    gz_count, col_count, slab_depth, half_x, width_y, rows = sizes
    full_x = half_x * col_count
    copies = 2 * PIECES + 4 + 3
    shape = jax.ShapeDtypeStruct(velocity.shape, jnp.float32)
    half = (3, half_x, slab_depth * width_y)
    vmem = pl.BlockSpec(memory_space=pltpu.VMEM)
    anywhere = pl.BlockSpec(memory_space=pltpu.HBM)
    own, incoming, after = pl.pallas_call(
        functools.partial(kernel, sizes),
        out_shape=(pltpu.VMEM(half, jnp.float32), pltpu.VMEM(half, jnp.float32), pltpu.VMEM(velocity.shape, jnp.float32)),
        in_specs=[anywhere] * 7,
        out_specs=(vmem,) * 3,
        scratch_shapes=[
            pltpu.VMEM((2,) + forces.shape, jnp.float32),
            pltpu.VMEM((3, rows, LANES), jnp.int32),
            pltpu.SMEM((1,), jnp.int32),
            pltpu.VMEM((2 * PIECES, 9 * rows // 2, LANES), jnp.float32),
            pltpu.VMEM(((11 + slab_depth) * rows, LANES), jnp.float32),
            pltpu.VMEM((3 * full_x, slab_depth * width_y), jnp.float32),
            pltpu.VMEM((2,) + velocity.shape[1:], jnp.float32),
            pltpu.VMEM((2, slab_depth, 3, SUBLANES, width_y), jnp.float32),
            pltpu.VMEM(velocity.shape, jnp.float32),
            pltpu.SemaphoreType.DMA((7,)),
            pltpu.SemaphoreType.DMA((copies,)),
            pltpu.SemaphoreType.DMA((copies,)),
        ],
        compiler_params=pltpu.CompilerParams(
            collective_id=0, has_side_effects=True, vmem_limit_bytes=56 * 1024 * 1024
        ),
    )(
        forces,
        offsets,
        cell_x.reshape(rows, LANES),
        cell_y.reshape(rows, LANES),
        cell_z.reshape(rows, LANES),
        band_start,
        velocity,
    )
    return pl.pallas_call(
        finish,
        out_shape=(shape, shape),
        in_specs=[vmem] * 3,
        out_specs=(anywhere,) * 2,
        scratch_shapes=[
            pltpu.VMEM(velocity.shape, jnp.float32),
            pltpu.VMEM(velocity.shape, jnp.float32),
            pltpu.SemaphoreType.DMA((2, slab_depth)),
        ],
        compiler_params=pltpu.CompilerParams(vmem_limit_bytes=16 * 1024 * 1024),
    )(own, incoming, after)


def solution(mesh):
    from_shapes = functools.partial(sized, mesh)
    in_specs = (
        P("gz", None, "col", None),
        P(None, ("gz", "col")),
        P(None, ("gz", "col")),
        P(("gz", "col")),
        P(("gz", "col")),
        P(("gz", "col")),
        P("gz"),
    )
    out_specs = (P("gz", None, "col", None), P("gz", None, "col", None))
    return jax.shard_map(
        from_shapes, mesh=mesh, in_specs=in_specs, out_specs=out_specs, check_vma=False
    )


def sized(mesh, velocity, forces, offsets, cell_x, cell_y, cell_z, band_start):
    slab_depth, _, half_x, width_y = velocity.shape
    rows = cell_x.shape[0] // LANES
    sizes = (mesh.shape["gz"], mesh.shape["col"], slab_depth, half_x, width_y, rows)
    return on_device(sizes, velocity, forces, offsets, cell_x, cell_y, cell_z, band_start)
```
